256 devices in a mesh: req: 64 (over y_lo, x, z), tp: 4 (over y_hi, core).
Axes of the slice: x: 4, y: 4 (y_hi: 2, y_lo: 2; y = y_hi * 2 + y_lo), z: 8, core: 2. Of those that a mesh axis runs over, the one named last changes fastest.
Arguments:
- hidden_in: bfloat16 [128, 256, 2048], P('req', None, 'tp'), may hold values from -6 to 6
- norm_gain: float32 [2048], replicated, may hold values from 0.1 to 1.9
- q_weight: bfloat16 [2048, 2048], P(None, 'tp'), may hold values from -0.125 to 0.125
- kv_weight: bfloat16 [2048, 1024], P(None, 'tp'), may hold values from -0.125 to 0.125
- out_weight: bfloat16 [2048, 2048], P('tp'), may hold values from -3 to 3
- post_gain: float32 [2048], P('tp'), may hold values from 0.1 to 1.9
- sink_cache: bfloat16 [128, 2, 4, 512], P('req'), may hold values from -16 to 16
- window_cache: bfloat16 [128, 2, 512, 512], P('req', None, 'tp'), may hold values from -320 to 320, as said below
- cached_len: int32 [128], P('req'), may hold values from 16 to 32768, as said below
- span_len: int32 [128], P('req'), may hold values from 1 to 256, as said below
- sink_count: int32 [128], P('req'), may hold values from 1 to 4, as said below
- window_size: int32 [128], P('req'), may hold values from 128 to 512, as said below
Outputs:
- layer_out: bfloat16 [128, 256, 2048], P('req', None, 'tp')
The draws below stay inside these ranges and needn't reach their ends.
Inputs may be any that keep to these rules, and one draw needn't show every extreme that they name: `window_cache`: slot s of request r holds the rotated key (entries below 256) and the value of position cached_len[r] - 512 + s. `cached_len`: one request has exactly 32768 cached tokens. Rows at or past span_len are padding; some request fills all 256. `sink_count`: some request keeps all 4. `window_size`: some request uses 512.
All inputs are finite; a program needn't handle non-finite values.
Results may differ from the reference program's by a relative error of at most 0.019.
Values may be sent and summed in bfloat16 or wider, within the bound.
A program may use at most 128 MiB of HBM per device.

```python
import math
import jax
import jax.numpy as jnp
from jax import lax

D = 2048
HEADS = 8
KVH = 2
HD = 256
WIN = 512
SINK = 4
MAXLEN = 32768
SPAN = 256
REQUESTS = 128


def place_top(key, values, top_value):
    spot = jax.random.randint(jax.random.fold_in(key, 91), (), 0, values.shape[0])
    return values.at[spot].set(top_value).astype(jnp.int32)


def draw_out_weight(key, part):
    column = jnp.arange(D, dtype=jnp.float32) / D
    rough = jax.random.uniform(jax.random.fold_in(key, 7), (1, D), jnp.float32, 0.7, 1.4)
    rising = jnp.exp(column * math.log(8.0))[None, :]
    base = jnp.clip(jax.random.normal(jax.random.fold_in(key, 3), (HEADS * HD, D), jnp.float32), -6.0, 6.0)
    return (base * rising * rough * (1.0 / math.sqrt(HEADS * HD))).astype(jnp.bfloat16)


def draw_window_cache(key, part):
    base = jax.random.normal(jax.random.fold_in(key, 3), (REQUESTS, KVH, WIN, 2 * HD), jnp.float32)
    return jnp.clip(base, -6.0, 6.0).astype(jnp.bfloat16)


def draw_cached_len(key, part):
    spread = jax.random.randint(jax.random.fold_in(key, 1), (REQUESTS,), 1, MAXLEN - 15)
    extra_len = jax.random.randint(jax.random.fold_in(key, 2), (REQUESTS,), 0, spread)
    return place_top(key, 16 + extra_len, MAXLEN)


def draw_span_len(key, part):
    values = jax.random.randint(jax.random.fold_in(key, 1), (REQUESTS,), 1, SPAN + 1)
    return place_top(key, values, SPAN)


def draw_sink_count(key, part):
    values = jax.random.randint(jax.random.fold_in(key, 1), (REQUESTS,), 1, SINK + 1)
    return place_top(key, values, SINK)


def draw_window_size(key, part):
    values = jax.random.randint(jax.random.fold_in(key, 1), (REQUESTS,), WIN // 4, WIN + 1)
    return place_top(key, values, WIN)


def block_levels(key, dims, shards, smallest, high):
    gain = 1.0
    for position, parts in shards:
        heights = jax.random.uniform(jax.random.fold_in(jax.random.fold_in(key, 6), position), (parts,), jnp.float32, smallest / len(shards), high / len(shards))
        gain = gain * jnp.repeat(jnp.exp(heights), dims[position] // parts).reshape((-1,) + (1,) * (len(dims) - 1 - position))
    return gain


def centred(key, dims, scale, most, cuts=(), held_as=jnp.bfloat16):
    values = scale * jax.random.normal(key, dims, jnp.float32)
    if cuts:
        values = values * block_levels(key, dims, cuts, -0.22, 0.18)
    return jnp.clip(values, -most, most).astype(held_as)


def setup_inputs(seed: int = 0) -> dict:
    splits = jax.random.split(jax.random.key(seed), 13)
    return {
        "hidden_in": centred(splits[0], (REQUESTS, SPAN, D), 1.0, 6.0, ((0, 64), (2, 4))),
        "norm_gain": jnp.clip(1.0 + 0.18 * jax.random.normal(splits[1], (D,), jnp.float32), 0.1, 1.9),
        "q_weight": centred(splits[2], (D, HEADS * HD), D ** -0.5, 0.125, ((1, 4),)),
        "kv_weight": centred(splits[3], (D, 2 * KVH * HD), D ** -0.5, 0.125, ((1, 4),)),
        "out_weight": draw_out_weight(jax.random.fold_in(splits[12], 71), 0),
        "post_gain": jnp.clip(1.0 + 0.18 * jax.random.normal(splits[5], (D,), jnp.float32), 0.1, 1.9),
        "sink_cache": centred(splits[6], (REQUESTS, KVH, SINK, 2 * HD), 3.0, 16.0, ((0, 64),)),
        "window_cache": draw_window_cache(jax.random.fold_in(splits[12], 71), 0),
        "cached_len": draw_cached_len(jax.random.fold_in(splits[12], 71), 0),
        "span_len": draw_span_len(jax.random.fold_in(splits[12], 71), 0),
        "sink_count": draw_sink_count(jax.random.fold_in(splits[12], 71), 0),
        "window_size": draw_window_size(jax.random.fold_in(splits[12], 71), 0),
    }


EPS = 1e-06
NEG = -1e+30

def rotate(block_rows, positions):
    half_size = block_rows.shape[-1] // 2
    frequency = jnp.exp(jnp.arange(half_size, dtype=jnp.float32) * (-2.0 * math.log(10000.0) / block_rows.shape[-1]))
    angles = positions.astype(jnp.float32)[..., None] * frequency
    cosine = jnp.cos(angles)[..., None, :]
    sine_part = jnp.sin(angles)[..., None, :]
    first_half = block_rows[..., :half_size]
    second_half = block_rows[..., half_size:]
    return jnp.concatenate([first_half * cosine - second_half * sine_part, second_half * cosine + first_half * sine_part], axis=-1)

def reference(hidden_in, norm_gain, q_weight, kv_weight, out_weight, post_gain, sink_cache, window_cache, cached_len, span_len, sink_count, window_size):
    groups = HEADS // KVH
    scaling = 1.0 / math.sqrt(HD)

    def one_request(request_items):
        row_block, sink_rows, window_rows, cached, fresh_count, sinks_kept, reach_len = request_items
        widened = row_block.astype(jnp.float32)
        normed = (widened * lax.rsqrt(lax.optimization_barrier(jnp.mean(widened * widened, axis=-1, keepdims=True)) + EPS) * norm_gain).astype(jnp.bfloat16)
        row_index = jnp.arange(SPAN, dtype=jnp.int32)
        positions = cached + row_index
        queries = jnp.dot(normed, q_weight, preferred_element_type=jnp.float32).reshape(SPAN, HEADS, HD)
        queries = rotate(queries, positions).astype(jnp.bfloat16)
        pair_rows = jnp.dot(normed, kv_weight, preferred_element_type=jnp.float32).reshape(SPAN, KVH, 2, HD)
        new_keys = rotate(pair_rows[:, :, 0, :], positions).astype(jnp.bfloat16)
        new_values = pair_rows[:, :, 1, :].astype(jnp.bfloat16)
        keys = jnp.concatenate([sink_rows[:, :, :HD], window_rows[:, :, :HD], jnp.transpose(new_keys, (1, 0, 2))], axis=1)
        values = jnp.concatenate([sink_rows[:, :, HD:], window_rows[:, :, HD:], jnp.transpose(new_values, (1, 0, 2))], axis=1)
        sink_mask = jnp.broadcast_to((jnp.arange(SINK, dtype=jnp.int32) < sinks_kept)[None, :], (SPAN, SINK))
        slot_pos = cached - WIN + jnp.arange(WIN, dtype=jnp.int32)
        pos_gap = positions[:, None] - slot_pos[None, :]
        window_mask = (slot_pos >= sinks_kept)[None, :] & (pos_gap < reach_len)
        step_gap = row_index[:, None] - row_index[None, :]
        span_mask = (step_gap >= 0) & (step_gap < reach_len) & (row_index < fresh_count)[None, :]
        key_mask = jnp.concatenate([sink_mask, window_mask, span_mask], axis=1)
        grouped = queries.reshape(SPAN, KVH, groups, HD).astype(jnp.float32)
        scores = jnp.einsum('cvgd,vsd->vgcs', grouped, keys.astype(jnp.float32)) * scaling
        scores = jnp.where(key_mask[None, None], scores, NEG)
        row_max = lax.optimization_barrier(jnp.max(scores, axis=-1, keepdims=True))
        weights = jnp.where(key_mask[None, None], jnp.exp(scores - row_max), 0.0)
        row_total = lax.optimization_barrier(jnp.sum(weights, axis=-1))
        rounded = lax.optimization_barrier(weights.astype(jnp.bfloat16)).astype(jnp.float32)
        mixed = jnp.einsum('vgcs,vsd->cvgd', rounded, values.astype(jnp.float32))
        mixed = mixed / jnp.transpose(row_total, (2, 0, 1))[..., None]
        attended = mixed.reshape(SPAN, HEADS * HD).astype(jnp.bfloat16)
        projected = jnp.dot(attended, out_weight, preferred_element_type=jnp.float32)
        square = lax.optimization_barrier(jnp.mean(projected * projected, axis=-1, keepdims=True))
        return (widened + post_gain * projected * lax.rsqrt(square + EPS)).astype(jnp.bfloat16)
    return lax.map(one_request, (hidden_in, sink_cache, window_cache, cached_len, span_len, sink_count, window_size))
```

```python
import math

import jax
import jax.numpy as jnp
from jax import lax
from jax.experimental import pallas as pl
from jax.experimental.pallas import tpu as pltpu
from jax.sharding import PartitionSpec as P

D = 2048
HEADS = 8
KVH = 2
HD = 256
WIN = 512
SINK = 4
SPAN = 256
EPS = 1e-06
NEG = -1e30

REQ = 2
TP = 4
FEAT = D // TP
SLOTS = WIN // TP
HALF = SPAN // 2
COLS = WIN + SPAN + 128
MESH = pl.DeviceIdType.MESH
F32 = jnp.float32
BF16 = jnp.bfloat16


def layer_kernel(
    cached_ref,
    span_ref,
    sinkn_ref,
    reach_ref,
    hid,
    ng,
    qw,
    kvw,
    ow,
    pg,
    sink,
    win,
    out,
    xg,
    wq,
    wkv,
    wo,
    gain,
    pgain,
    sinkb,
    kvb,
    qb,
    biasb,
    cosb,
    sinb,
    attb,
    ownb,
    sendb,
    recvb,
    ssb,
    outb,
    lsem,
    osem,
    ssem,
    rsem,
):
    r = lax.axis_index("req")
    t = lax.axis_index("tp")
    core = lax.rem(t, 2)
    chip = lax.div(t, 2)
    other = 1 - chip
    tc = 2 * chip + 1 - core
    to = 2 * other + core
    tx = 2 * other + 1 - core

    def columns(i):
        return pl.ds(pl.multiple_of(i * FEAT, FEAT), FEAT)

    def slots(i):
        return pl.ds(pl.multiple_of(i * SLOTS, SLOTS), SLOTS)

    local = {}

    def fetch(name, src, dst):
        copy = pltpu.make_async_copy(src, dst, lsem.at[len(local)])
        copy.start()
        local[name] = copy

    remote = {}

    def make(name, src, dst, target):
        i = len(remote)
        remote[name] = pltpu.make_async_remote_copy(
            src_ref=src,
            dst_ref=dst,
            send_sem=ssem.at[i],
            recv_sem=rsem.at[i],
            device_id=(r, target),
            device_id_type=MESH,
        )
        return remote[name]

    fetch("gain", ng, gain)
    for q in range(REQ):
        fetch(("hid", q), hid.at[q], xg.at[q, t])
    fetch("wq", qw, wq)
    fetch("wkv", kvw, wkv)
    for q in range(REQ):
        for k in range(2):
            fetch(
                ("win", q, k),
                win.at[q, chip, :, k * HD : (k + 1) * HD],
                kvb.at[k, q, slots(t)],
            )
    fetch("sink", sink.at[:, chip], sinkb)
    fetch("wo0", ow.at[:, columns(t)], wo.at[core, 0])
    fetch("wo1", ow.at[:, columns(to)], wo.at[core, 1])
    fetch("pg", pg, pgain)

    barrier = pltpu.get_barrier_semaphore()
    for peer in (tc, to, tx):
        pl.semaphore_signal(barrier, inc=1, device_id=(r, peer), device_id_type=MESH)
    pl.semaphore_wait(barrier, 3)

    pieces = [(q, h) for q in range(REQ) for h in range(2)]
    for q in range(REQ):
        for h in range(2):
            rows = pl.ds(h * HALF, HALF)
            make(("H", q, h), hid.at[q, rows], xg.at[q, t, rows], to).start()
        make(("D", q), hid.at[q], xg.at[q, t], tc).start()
        for k in range(2):
            lanes = slice(k * HD, (k + 1) * HD)
            make(("C", q, k), win.at[q, other, :, lanes], kvb.at[k, q, slots(t)], to).start()
    for q in range(REQ):
        for k in range(2):
            lanes = slice(k * HD, (k + 1) * HD)
            make(("E", q, k), win.at[q, chip, :, lanes], kvb.at[k, q, slots(t)], tc).start()
    make(("W", 0), ow.at[:, columns(tc)], wo.at[core, 0], tc).start()
    make(("W", 1), ow.at[:, columns(tx)], wo.at[core, 1], tc).start()
    for q, h in pieces:
        rows = pl.ds(h * HALF, HALF)
        make(("HF", q, h), xg.at[q, to, rows], xg.at[q, to, rows], tc)
        new_rows = pl.ds(WIN + h * HALF, HALF)
        make(("N", q, h), kvb.at[core, q, new_rows], kvb.at[core, q, new_rows], tc)
        make(("A", q, h), attb.at[q, core, rows], attb.at[q, core, rows], tc)
        make(("O", q, h), sendb.at[q, h], recvb.at[q, h], to)
        for name, peer in (("c", tc), ("o", to), ("x", tx)):
            make(("S" + name, q, h), ssb.at[q, h, t], ssb.at[q, h, t], peer)
    for q in range(REQ):
        for k in range(2):
            make(("CF", q, k), kvb.at[k, q, slots(to)], kvb.at[k, q, slots(to)], tc)

    lane = lax.broadcasted_iota(jnp.int32, (HALF, HD // 2), 1).astype(F32)
    frequency = jnp.exp(lane * (-2.0 * math.log(10000.0) / HD))
    for q, h in pieces:
        row = lax.broadcasted_iota(jnp.int32, (HALF, HD // 2), 0) + h * HALF
        angles = (row + cached_ref[q]).astype(F32) * frequency
        cosb[q, h] = jnp.cos(angles)
        sinb[q, h] = jnp.sin(angles)
    for q, h in pieces:
        cached, fresh, sinks, reach = cached_ref[q], span_ref[q], sinkn_ref[q], reach_ref[q]
        row = lax.broadcasted_iota(jnp.int32, (HALF, WIN), 0) + h * HALF
        col = lax.broadcasted_iota(jnp.int32, (HALF, WIN), 1)
        allowed = (col >= sinks + WIN - cached) & (row + WIN - col < reach)
        biasb[q, h, :, 0:WIN] = jnp.where(allowed, 0.0, NEG)
        row = lax.broadcasted_iota(jnp.int32, (HALF, SPAN), 0) + h * HALF
        col = lax.broadcasted_iota(jnp.int32, (HALF, SPAN), 1)
        allowed = (col <= row) & (col < fresh) & (row - col < reach)
        biasb[q, h, :, WIN : WIN + SPAN] = jnp.where(allowed, 0.0, NEG)
        col = lax.broadcasted_iota(jnp.int32, (HALF, 128), 1)
        biasb[q, h, :, WIN + SPAN : COLS] = jnp.where(col < sinks, 0.0, NEG)
    local["sink"].wait()
    for q in range(REQ):
        for k in range(2):
            kvb[k, q, WIN + SPAN : COLS, :] = jnp.zeros((COLS - WIN - SPAN, HD), BF16)
            kvb[k, q, WIN + SPAN : WIN + SPAN + SINK, :] = sinkb[q, :, k * HD : (k + 1) * HD]
    local["gain"].wait()
    local["wq"].wait()
    local["wkv"].wait()

    def pass_on(q, h):
        remote["H", q, h].wait_recv()
        remote["HF", q, h].start()

    def pass_cache(q):
        for k in range(2):
            remote["C", q, k].wait_recv()
            remote["CF", q, k].start()

    def project(q, h):
        rows = slice(h * HALF, (h + 1) * HALF)
        if h == 0:
            local["hid", q].wait()
            remote["D", q].wait_recv()
        remote["HF", q, h].wait_recv()
        square = jnp.zeros((HALF, 1), F32)
        acc_q = jnp.zeros((HALF, 2 * HD), F32)
        acc_kv = jnp.zeros((HALF, HD), F32)
        for s in range(TP):
            span = slice(s * FEAT, (s + 1) * FEAT)
            x = xg[q, s, rows, :].astype(F32)
            square += jnp.sum(x * x, axis=-1, keepdims=True)
            scaled = (x * gain[:, span]).astype(BF16)
            acc_q += jnp.dot(scaled, wq[span, :], preferred_element_type=F32)
            acc_kv += jnp.dot(scaled, wkv[span, :], preferred_element_type=F32)
        scale = lax.rsqrt(square * (1.0 / D) + EPS)
        cosine, sine = cosb[q, h], sinb[q, h]
        cosine, sine = cosine * scale, sine * scale
        u, w = acc_kv[:, : HD // 2], acc_kv[:, HD // 2 :]
        is_key = core == 0
        cos_kv = jnp.where(is_key, cosine, jnp.broadcast_to(scale, cosine.shape))
        sin_kv = jnp.where(is_key, sine, 0.0)
        new_rows = slice(WIN + h * HALF, WIN + (h + 1) * HALF)
        kvb[core, q, new_rows, : HD // 2] = (u * cos_kv - w * sin_kv).astype(BF16)
        kvb[core, q, new_rows, HD // 2 :] = (w * cos_kv + u * sin_kv).astype(BF16)
        remote["N", q, h].start()
        cosine, sine = cosine * (1.0 / math.sqrt(HD)), sine * (1.0 / math.sqrt(HD))
        for n in range(2):
            u = acc_q[:, n * HD : n * HD + HD // 2]
            w = acc_q[:, n * HD + HD // 2 : (n + 1) * HD]
            qb[q, h, n, :, : HD // 2] = (u * cosine - w * sine).astype(BF16)
            qb[q, h, n, :, HD // 2 :] = (w * cosine + u * sine).astype(BF16)

    def keys_ready(q):
        for k in range(2):
            local["win", q, k].wait()
            remote["E", q, k].wait_recv()
            remote["CF", q, k].wait_recv()
        for h in range(2):
            remote["N", q, h].wait_recv()

    def attend(q, h):
        query = qb[q, h].reshape(2 * HALF, HD)
        scores = lax.dot_general(
            query, kvb[0, q], (((1,), (1,)), ((), ())), preferred_element_type=F32
        )
        scores = scores.reshape(2, HALF, COLS) + biasb[q, h][None]
        peak = jnp.max(scores, axis=-1, keepdims=True)
        weights = jnp.exp(scores - peak)
        total = jnp.sum(weights, axis=-1, keepdims=True).reshape(2 * HALF, 1)
        weights = weights.astype(BF16).reshape(2 * HALF, COLS)
        mixed = jnp.dot(weights, kvb[1, q], preferred_element_type=F32) * (1.0 / total)
        mixed = mixed.astype(BF16)
        rows = slice(h * HALF, (h + 1) * HALF)
        for n in range(2):
            attb[q, core, rows, n * HD : (n + 1) * HD] = mixed[n * HALF : (n + 1) * HALF]
        remote["A", q, h].start()

    def emit(q, h):
        rows = slice(h * HALF, (h + 1) * HALF)
        remote["A", q, h].wait_recv()
        first, second = attb[q, 0, rows, :], attb[q, 1, rows, :]
        lent = jnp.dot(first, wo[0, 1], preferred_element_type=F32) + jnp.dot(
            second, wo[1, 1], preferred_element_type=F32
        )
        sendb[q, h] = lent.astype(BF16)
        remote["O", q, h].start()
        ownb[q, h] = jnp.dot(first, wo[0, 0], preferred_element_type=F32) + jnp.dot(
            second, wo[1, 0], preferred_element_type=F32
        )

    def squares(q, h):
        remote["O", q, h].wait_recv()
        projected = ownb[q, h] + recvb[q, h].astype(F32)
        ownb[q, h] = projected
        square = jnp.sum(projected * projected, axis=-1, keepdims=True)
        turned = jnp.transpose(jnp.broadcast_to(square, (HALF, 128)))
        ssb[q, h, t] = turned[0:8, :]
        for name in ("Sc", "So", "Sx"):
            remote[name, q, h].start()

    stores = []

    def finish(q, h):
        for name in ("Sc", "So", "Sx"):
            remote[name, q, h].wait_recv()
        square = ssb[q, h, 0] + ssb[q, h, 1] + ssb[q, h, 2] + ssb[q, h, 3]
        scale = lax.rsqrt(square * (1.0 / D) + EPS)
        scale = jnp.transpose(jnp.broadcast_to(scale[0:1, :], (128, HALF)))[:, 0:1]
        rows = slice(h * HALF, (h + 1) * HALF)
        kept = xg[q, t, rows, :].astype(F32)
        outb[q, rows, :] = (kept + pgain[...] * ownb[q, h] * scale).astype(BF16)
        copy = pltpu.make_async_copy(
            outb.at[q, pl.ds(h * HALF, HALF)],
            out.at[q, pl.ds(h * HALF, HALF)],
            osem.at[2 * q + h],
        )
        copy.start()
        stores.append(copy)

    pass_on(0, 0)
    project(0, 0)
    pass_on(0, 1)
    project(0, 1)
    pass_cache(0)
    keys_ready(0)
    attend(0, 0)
    attend(0, 1)
    pass_on(1, 0)
    for name in ("wo0", "wo1", "pg"):
        local[name].wait()
    for i in range(2):
        remote["W", i].wait_recv()
    emit(0, 0)
    emit(0, 1)
    pass_on(1, 1)
    project(1, 0)
    project(1, 1)
    pass_cache(1)
    keys_ready(1)
    attend(1, 0)
    attend(1, 1)
    emit(1, 0)
    emit(1, 1)
    squares(0, 0)
    squares(0, 1)
    finish(0, 0)
    finish(0, 1)
    squares(1, 0)
    squares(1, 1)
    finish(1, 0)
    finish(1, 1)
    for copy in remote.values():
        copy.wait_send()
    for copy in stores:
        copy.wait()


def per_device(
    hidden_in,
    norm_gain,
    q_weight,
    kv_weight,
    out_weight,
    post_gain,
    sink_cache,
    window_cache,
    cached_len,
    span_len,
    sink_count,
    window_size,
):
    anywhere = pl.BlockSpec(memory_space=pl.ANY)
    scalars = pl.BlockSpec(memory_space=pltpu.SMEM)
    copies = 52
    return pl.pallas_call(
        layer_kernel,
        out_shape=jax.ShapeDtypeStruct((REQ, SPAN, FEAT), BF16),
        in_specs=[scalars] * 4 + [anywhere] * 8,
        out_specs=anywhere,
        scratch_shapes=[
            pltpu.VMEM((REQ, TP, SPAN, FEAT), BF16),
            pltpu.VMEM((D, 2 * HD), BF16),
            pltpu.VMEM((D, HD), BF16),
            pltpu.VMEM((2, 2, 2 * HD, FEAT), BF16),
            pltpu.VMEM((1, D), F32),
            pltpu.VMEM((1, FEAT), F32),
            pltpu.VMEM((REQ, SINK, 2 * HD), BF16),
            pltpu.VMEM((2, REQ, COLS, HD), BF16),
            pltpu.VMEM((REQ, 2, 2, HALF, HD), BF16),
            pltpu.VMEM((REQ, 2, HALF, COLS), F32),
            pltpu.VMEM((REQ, 2, HALF, HD // 2), F32),
            pltpu.VMEM((REQ, 2, HALF, HD // 2), F32),
            pltpu.VMEM((REQ, 2, SPAN, 2 * HD), BF16),
            pltpu.VMEM((REQ, 2, HALF, FEAT), F32),
            pltpu.VMEM((REQ, 2, HALF, FEAT), BF16),
            pltpu.VMEM((REQ, 2, HALF, FEAT), BF16),
            pltpu.VMEM((REQ, 2, TP, 8, HALF), F32),
            pltpu.VMEM((REQ, SPAN, FEAT), BF16),
            pltpu.SemaphoreType.DMA((16,)),
            pltpu.SemaphoreType.DMA((4,)),
            pltpu.SemaphoreType.DMA((copies,)),
            pltpu.SemaphoreType.DMA((copies,)),
        ],
        compiler_params=pltpu.CompilerParams(
            collective_id=0, has_side_effects=True, vmem_limit_bytes=60 * 2**20
        ),
    )(
        cached_len,
        span_len,
        sink_count,
        window_size,
        hidden_in,
        norm_gain.reshape(1, D),
        q_weight,
        kv_weight,
        out_weight,
        post_gain.reshape(1, FEAT),
        sink_cache,
        window_cache,
    )


def solution(mesh):
    in_specs = (
        P("req", None, "tp"),
        P(),
        P(None, "tp"),
        P(None, "tp"),
        P("tp", None),
        P("tp"),
        P("req", None, None, None),
        P("req", None, "tp", None),
        P("req"),
        P("req"),
        P("req"),
        P("req"),
    )
    return jax.shard_map(
        per_device,
        mesh=mesh,
        in_specs=in_specs,
        out_specs=P("req", None, "tp"),
        check_vma=False,
    )
```

```python
import math

import jax
import jax.numpy as jnp
from jax import lax
from jax.experimental import pallas as pl
from jax.experimental.pallas import tpu as pltpu
from jax.sharding import PartitionSpec as P

D = 2048
HEADS = 8
KVH = 2
HD = 256
WIN = 512
SINK = 4
SPAN = 256
EPS = 1e-06
NEG = -1e30

REQ = 2
TP = 4
FEAT = D // TP
SLOTS = WIN // TP
HALF = SPAN // 2
PAD = 128
NEW = PAD + WIN
COLS = NEW + SPAN
OUTS = ((0, 0, 0, HALF), (0, 1, 0, HALF), (1, 0, 0, HALF)) + tuple(
    (1, 1, i * 32, 32) for i in range(4)
)
MESH = pl.DeviceIdType.MESH
F32 = jnp.float32
BF16 = jnp.bfloat16


def layer_kernel(
    cached_in,
    span_in,
    sinkn_in,
    reach_in,
    hid,
    ng,
    qw,
    kvw,
    ow,
    pg,
    sink,
    win,
    out,
    cached_ref,
    span_ref,
    sinkn_ref,
    reach_ref,
    xg,
    wq,
    wkv,
    wo,
    gain,
    pgain,
    sinkb,
    kvb,
    qb,
    biasb,
    cosb,
    sinb,
    attb,
    ownb,
    sendb,
    recvb,
    ssb,
    outb,
    lsem,
    osem,
    ssem,
    rsem,
):
    r = lax.axis_index("req")
    t = lax.axis_index("tp")
    core = lax.rem(t, 2)
    chip = lax.div(t, 2)
    other = 1 - chip
    tc = 2 * chip + 1 - core
    to = 2 * other + core
    tx = 2 * other + 1 - core

    barrier = pltpu.get_barrier_semaphore()
    for peer in (to, tx, tc):
        pl.semaphore_signal(barrier, inc=1, device_id=(r, peer), device_id_type=MESH)

    def columns(i):
        return pl.ds(pl.multiple_of(i * FEAT, FEAT), FEAT)

    def slots(i):
        return pl.ds(pl.multiple_of(PAD + i * SLOTS, SLOTS), SLOTS)

    local = {}

    def fetch(name, src, dst):
        copy = pltpu.make_async_copy(src, dst, lsem.at[len(local)])
        copy.start()
        local[name] = copy

    remote = {}

    def make(name, src, dst, target):
        i = len(remote)
        remote[name] = pltpu.make_async_remote_copy(
            src_ref=src,
            dst_ref=dst,
            send_sem=ssem.at[i],
            recv_sem=rsem.at[i],
            device_id=(r, target),
            device_id_type=MESH,
        )
        return remote[name]

    fetch("cached", cached_in, cached_ref)
    fetch("span", span_in, span_ref)
    fetch("sinkn", sinkn_in, sinkn_ref)
    fetch("reach", reach_in, reach_ref)
    fetch("gain", ng, gain)
    for q in range(REQ):
        fetch(("hid", q), hid.at[q], xg.at[q, t])
    fetch("wq", qw, wq)
    fetch("wkv", kvw, wkv)
    for q in range(REQ):
        for k in range(2):
            fetch(
                ("win", q, k),
                win.at[q, chip, :, k * HD : (k + 1) * HD],
                kvb.at[k, q, slots(t)],
            )
    fetch("sink", sink.at[:, chip], sinkb)
    fetch("wo0", ow.at[:, columns(t)], wo.at[core, 0])
    fetch("wo1", ow.at[:, columns(to)], wo.at[core, 1])
    fetch("pg", pg, pgain)

    pl.semaphore_wait(barrier, 3)

    pieces = [(q, h) for q in range(REQ) for h in range(2)]

    def send_rows(q, h):
        rows = pl.ds(h * HALF, HALF)
        make(("H", q, h), hid.at[q, rows], xg.at[q, t, rows], to).start()

    def send_cache(q):
        for k in range(2):
            lanes = slice(k * HD, (k + 1) * HD)
            make(("C", q, k), win.at[q, other, :, lanes], kvb.at[k, q, slots(t)], to).start()

    send_rows(0, 0)
    send_rows(0, 1)
    send_cache(0)
    send_rows(1, 0)
    send_cache(1)
    send_rows(1, 1)
    for q in range(REQ):
        make(("D", q), hid.at[q], xg.at[q, t], tc).start()
    for q in range(REQ):
        for k in range(2):
            lanes = slice(k * HD, (k + 1) * HD)
            make(("E", q, k), win.at[q, chip, :, lanes], kvb.at[k, q, slots(t)], tc).start()
    make(("W", 0), ow.at[:, columns(tc)], wo.at[core, 0], tc).start()
    make(("W", 1), ow.at[:, columns(tx)], wo.at[core, 1], tc).start()
    for q, h in pieces:
        rows = pl.ds(h * HALF, HALF)
        make(("HF", q, h), xg.at[q, to, rows], xg.at[q, to, rows], tc)
        new_rows = pl.ds(NEW + h * HALF, HALF)
        make(("N", q, h), kvb.at[core, q, new_rows], kvb.at[core, q, new_rows], tc)
        make(("A", q, h), attb.at[q, core, rows], attb.at[q, core, rows], tc)
    for i, (q, h, first, count) in enumerate(OUTS):
        rows = pl.ds(first, count)
        make(("O", i), sendb.at[q, h, rows], recvb.at[q, h, rows], to)
        for name, peer in (("o", to), ("x", tx), ("c", tc)):
            make(("S" + name, i), ssb.at[i, t], ssb.at[i, t], peer)
    for q in range(REQ):
        for k in range(2):
            make(("CF", q, k), kvb.at[k, q, slots(to)], kvb.at[k, q, slots(to)], tc)

    for name in ("cached", "span", "sinkn", "reach"):
        local[name].wait()
    lane = lax.broadcasted_iota(jnp.int32, (HALF, HD // 2), 1).astype(F32)
    frequency = jnp.exp(lane * (-2.0 * math.log(10000.0) / HD))
    for q, h in pieces:
        row = lax.broadcasted_iota(jnp.int32, (HALF, HD // 2), 0) + h * HALF
        angles = (row + cached_ref[q]).astype(F32) * frequency
        cosb[q, h] = jnp.cos(angles)
        sinb[q, h] = jnp.sin(angles)
    for q, h in pieces:
        cached, fresh, sinks, reach = cached_ref[q], span_ref[q], sinkn_ref[q], reach_ref[q]
        row = lax.broadcasted_iota(jnp.int32, (HALF, WIN), 0) + h * HALF
        col = lax.broadcasted_iota(jnp.int32, (HALF, WIN), 1)
        allowed = (col >= sinks + WIN - cached) & (row + WIN - col < reach)
        biasb[q, h, :, PAD:NEW] = jnp.where(allowed, 0.0, NEG)
        row = lax.broadcasted_iota(jnp.int32, (HALF, SPAN), 0) + h * HALF
        col = lax.broadcasted_iota(jnp.int32, (HALF, SPAN), 1)
        allowed = (col <= row) & (col < fresh) & (row - col < reach)
        biasb[q, h, :, NEW:COLS] = jnp.where(allowed, 0.0, NEG)
        col = lax.broadcasted_iota(jnp.int32, (HALF, PAD), 1)
        biasb[q, h, :, 0:PAD] = jnp.where(col < jnp.minimum(sinks, SINK), 0.0, NEG)
    local["sink"].wait()
    for q in range(REQ):
        for k in range(2):
            kvb[k, q, 0:PAD, :] = jnp.zeros((PAD, HD), BF16)
            kvb[k, q, 0:SINK, :] = sinkb[q, :, k * HD : (k + 1) * HD]
    local["gain"].wait()
    local["wq"].wait()
    local["wkv"].wait()

    def pass_on(q, h):
        remote["H", q, h].wait_recv()
        remote["HF", q, h].start()

    def pass_cache(q):
        for k in range(2):
            remote["C", q, k].wait_recv()
            remote["CF", q, k].start()

    def project(q, h):
        rows = slice(h * HALF, (h + 1) * HALF)
        if h == 0:
            local["hid", q].wait()
            remote["D", q].wait_recv()
        remote["HF", q, h].wait_recv()
        square = jnp.zeros((HALF, 1), F32)
        acc_q = jnp.zeros((HALF, 2 * HD), F32)
        acc_kv = jnp.zeros((HALF, HD), F32)
        for s in range(TP):
            span = slice(s * FEAT, (s + 1) * FEAT)
            x = xg[q, s, rows, :].astype(F32)
            square += jnp.sum(x * x, axis=-1, keepdims=True)
            scaled = (x * gain[:, span]).astype(BF16)
            acc_q += jnp.dot(scaled, wq[span, :], preferred_element_type=F32)
            acc_kv += jnp.dot(scaled, wkv[span, :], preferred_element_type=F32)
        scale = lax.rsqrt(square * (1.0 / D) + EPS)
        cosine, sine = cosb[q, h], sinb[q, h]
        cosine, sine = cosine * scale, sine * scale
        u, w = acc_kv[:, : HD // 2], acc_kv[:, HD // 2 :]
        is_key = core == 0
        cos_kv = jnp.where(is_key, cosine, jnp.broadcast_to(scale, cosine.shape))
        sin_kv = jnp.where(is_key, sine, 0.0)
        new_rows = slice(NEW + h * HALF, NEW + (h + 1) * HALF)
        kvb[core, q, new_rows, : HD // 2] = (u * cos_kv - w * sin_kv).astype(BF16)
        kvb[core, q, new_rows, HD // 2 :] = (w * cos_kv + u * sin_kv).astype(BF16)
        remote["N", q, h].start()
        cosine, sine = cosine * (1.0 / math.sqrt(HD)), sine * (1.0 / math.sqrt(HD))
        for n in range(2):
            u = acc_q[:, n * HD : n * HD + HD // 2]
            w = acc_q[:, n * HD + HD // 2 : (n + 1) * HD]
            qb[q, h, n, :, : HD // 2] = (u * cosine - w * sine).astype(BF16)
            qb[q, h, n, :, HD // 2 :] = (w * cosine + u * sine).astype(BF16)

    def keys_ready(q):
        for k in range(2):
            local["win", q, k].wait()
            remote["E", q, k].wait_recv()
            remote["CF", q, k].wait_recv()

    def attend(q, h):
        remote["N", q, h].wait_recv()
        cols = NEW + (h + 1) * HALF
        query = qb[q, h].reshape(2 * HALF, HD)
        scores = lax.dot_general(
            query, kvb[0, q, :cols], (((1,), (1,)), ((), ())), preferred_element_type=F32
        )
        scores = scores.reshape(2, HALF, cols) + biasb[q, h, :, :cols][None]
        peak = jnp.max(scores, axis=-1, keepdims=True)
        weights = jnp.exp(scores - peak)
        total = jnp.sum(weights, axis=-1, keepdims=True).reshape(2 * HALF, 1)
        weights = weights.astype(BF16).reshape(2 * HALF, cols)
        mixed = jnp.dot(weights, kvb[1, q, :cols], preferred_element_type=F32) * (1.0 / total)
        mixed = mixed.astype(BF16)
        rows = slice(h * HALF, (h + 1) * HALF)
        for n in range(2):
            attb[q, core, rows, n * HD : (n + 1) * HD] = mixed[n * HALF : (n + 1) * HALF]
        remote["A", q, h].start()

    def emit(q, h):
        rows = slice(h * HALF, (h + 1) * HALF)
        remote["A", q, h].wait_recv()
        first, second = attb[q, 0, rows, :], attb[q, 1, rows, :]
        lent = jnp.dot(first, wo[0, 1], preferred_element_type=F32) + jnp.dot(
            second, wo[1, 1], preferred_element_type=F32
        )
        sendb[q, h] = lent.astype(BF16)
        for i, piece in enumerate(OUTS):
            if piece[:2] == (q, h):
                remote["O", i].start()
        ownb[q, h] = jnp.dot(first, wo[0, 0], preferred_element_type=F32) + jnp.dot(
            second, wo[1, 0], preferred_element_type=F32
        )

    def diagonal(count):
        row = lax.broadcasted_iota(jnp.int32, (count, 128), 0)
        return row == lax.broadcasted_iota(jnp.int32, (count, 128), 1)

    def squares(i):
        q, h, first, count = OUTS[i]
        rows = slice(first, first + count)
        remote["O", i].wait_recv()
        projected = ownb[q, h, rows, :] + recvb[q, h, rows, :].astype(F32)
        ownb[q, h, rows, :] = projected
        square = jnp.sum(projected * projected, axis=-1, keepdims=True)
        turned = jnp.sum(jnp.where(diagonal(count), square, 0.0), axis=0, keepdims=True)
        ssb[i, t] = jnp.broadcast_to(turned, (8, 128))
        for name in ("So", "Sx", "Sc"):
            remote[name, i].start()

    stores = []

    def finish(i):
        q, h, first, count = OUTS[i]
        for name in ("So", "Sx", "Sc"):
            remote[name, i].wait_recv()
        square = ssb[i, 0] + ssb[i, 1] + ssb[i, 2] + ssb[i, 3]
        scale = lax.rsqrt(square * (1.0 / D) + EPS)[0:1, :]
        scale = jnp.sum(jnp.where(diagonal(count), scale, 0.0), axis=-1, keepdims=True)
        rows = slice(h * HALF + first, h * HALF + first + count)
        kept = xg[q, t, rows, :].astype(F32)
        projected = ownb[q, h, first : first + count, :]
        outb[q, rows, :] = (kept + pgain[...] * projected * scale).astype(BF16)
        span = pl.ds(h * HALF + first, count)
        copy = pltpu.make_async_copy(outb.at[q, span], out.at[q, span], osem.at[i])
        copy.start()
        stores.append(copy)

    pass_on(0, 0)
    project(0, 0)
    pass_on(0, 1)
    project(0, 1)
    pass_cache(0)
    keys_ready(0)
    attend(0, 0)
    attend(0, 1)
    pass_on(1, 0)
    for name in ("wo0", "wo1", "pg"):
        local[name].wait()
    for i in range(2):
        remote["W", i].wait_recv()
    emit(0, 0)
    emit(0, 1)
    project(1, 0)
    pass_cache(1)
    keys_ready(1)
    attend(1, 0)
    pass_on(1, 1)
    emit(1, 0)
    project(1, 1)
    attend(1, 1)
    emit(1, 1)
    for i in range(len(OUTS)):
        squares(i)
        if i == 2:
            finish(0)
            finish(1)
    for i in range(2, len(OUTS)):
        finish(i)
    for copy in remote.values():
        copy.wait_send()
    for copy in stores:
        copy.wait()


def per_device(
    hidden_in,
    norm_gain,
    q_weight,
    kv_weight,
    out_weight,
    post_gain,
    sink_cache,
    window_cache,
    cached_len,
    span_len,
    sink_count,
    window_size,
):
    anywhere = pl.BlockSpec(memory_space=pl.ANY)
    copies = 70
    return pl.pallas_call(
        layer_kernel,
        out_shape=jax.ShapeDtypeStruct((REQ, SPAN, FEAT), BF16),
        in_specs=[anywhere] * 12,
        out_specs=anywhere,
        scratch_shapes=[
            pltpu.SMEM((REQ,), jnp.int32),
            pltpu.SMEM((REQ,), jnp.int32),
            pltpu.SMEM((REQ,), jnp.int32),
            pltpu.SMEM((REQ,), jnp.int32),
            pltpu.VMEM((REQ, TP, SPAN, FEAT), BF16),
            pltpu.VMEM((D, 2 * HD), BF16),
            pltpu.VMEM((D, HD), BF16),
            pltpu.VMEM((2, 2, 2 * HD, FEAT), BF16),
            pltpu.VMEM((1, D), F32),
            pltpu.VMEM((1, FEAT), F32),
            pltpu.VMEM((REQ, SINK, 2 * HD), BF16),
            pltpu.VMEM((2, REQ, COLS, HD), BF16),
            pltpu.VMEM((REQ, 2, 2, HALF, HD), BF16),
            pltpu.VMEM((REQ, 2, HALF, COLS), F32),
            pltpu.VMEM((REQ, 2, HALF, HD // 2), F32),
            pltpu.VMEM((REQ, 2, HALF, HD // 2), F32),
            pltpu.VMEM((REQ, 2, SPAN, 2 * HD), BF16),
            pltpu.VMEM((REQ, 2, HALF, FEAT), F32),
            pltpu.VMEM((REQ, 2, HALF, FEAT), BF16),
            pltpu.VMEM((REQ, 2, HALF, FEAT), BF16),
            pltpu.VMEM((len(OUTS), TP, 8, 128), F32),
            pltpu.VMEM((REQ, SPAN, FEAT), BF16),
            pltpu.SemaphoreType.DMA((20,)),
            pltpu.SemaphoreType.DMA((len(OUTS),)),
            pltpu.SemaphoreType.DMA((copies,)),
            pltpu.SemaphoreType.DMA((copies,)),
        ],
        compiler_params=pltpu.CompilerParams(
            collective_id=0, has_side_effects=True, vmem_limit_bytes=60 * 2**20
        ),
    )(
        cached_len,
        span_len,
        sink_count,
        window_size,
        hidden_in,
        norm_gain.reshape(1, D),
        q_weight,
        kv_weight,
        out_weight,
        post_gain.reshape(1, FEAT),
        sink_cache,
        window_cache,
    )


def solution(mesh):
    in_specs = (
        P("req", None, "tp"),
        P(),
        P(None, "tp"),
        P(None, "tp"),
        P("tp", None),
        P("tp"),
        P("req", None, None, None),
        P("req", None, "tp", None),
        P("req"),
        P("req"),
        P("req"),
        P("req"),
    )
    return jax.shard_map(
        per_device,
        mesh=mesh,
        in_specs=in_specs,
        out_specs=P("req", None, "tp"),
        check_vma=False,
    )
```

```python
import math

import jax
import jax.numpy as jnp
from jax import lax
from jax.experimental import pallas as pl
from jax.experimental.pallas import tpu as pltpu
from jax.sharding import PartitionSpec as P

D = 2048
HEADS = 8
KVH = 2
HD = 256
WIN = 512
SINK = 4
SPAN = 256
EPS = 1e-06
NEG = -1e30

REQ = 2
TP = 4
FEAT = D // TP
SLOTS = WIN // TP
HALF = SPAN // 2
PAD = 128
NEW = PAD + WIN
COLS = NEW + SPAN
OUTS = ((0, 0, 0, HALF), (0, 1, 0, HALF), (1, 0, 0, HALF)) + tuple(
    (1, 1, i * 32, 32) for i in range(4)
)
MESH = pl.DeviceIdType.MESH
F32 = jnp.float32
BF16 = jnp.bfloat16


def layer_kernel(
    cached_in,
    span_in,
    sinkn_in,
    reach_in,
    hid,
    ng,
    qw,
    kvw,
    ow,
    pg,
    sink,
    win,
    out,
    cached_ref,
    span_ref,
    sinkn_ref,
    reach_ref,
    xg,
    wq,
    wkv,
    wo,
    gain,
    pgain,
    sinkb,
    kvb,
    qb,
    biasb,
    cosb,
    sinb,
    attb,
    ownb,
    sendb,
    recvb,
    ssb,
    lsem,
    ssem,
    rsem,
):
    r = lax.axis_index("req")
    t = lax.axis_index("tp")
    core = lax.rem(t, 2)
    chip = lax.div(t, 2)
    other = 1 - chip
    tc = 2 * chip + 1 - core
    to = 2 * other + core
    tx = 2 * other + 1 - core

    barrier = pltpu.get_barrier_semaphore()
    for peer in (to, tx, tc):
        pl.semaphore_signal(barrier, inc=1, device_id=(r, peer), device_id_type=MESH)

    def columns(i):
        return pl.ds(pl.multiple_of(i * FEAT, FEAT), FEAT)

    def slots(i):
        return pl.ds(pl.multiple_of(PAD + i * SLOTS, SLOTS), SLOTS)

    local = {}

    def fetch(name, src, dst):
        copy = pltpu.make_async_copy(src, dst, lsem.at[len(local)])
        copy.start()
        local[name] = copy

    remote = {}

    def make(name, src, dst, target):
        i = len(remote)
        remote[name] = pltpu.make_async_remote_copy(
            src_ref=src,
            dst_ref=dst,
            send_sem=ssem.at[i],
            recv_sem=rsem.at[i],
            device_id=(r, target),
            device_id_type=MESH,
        )
        return remote[name]

    fetch("cached", cached_in, cached_ref)
    fetch("span", span_in, span_ref)
    fetch("sinkn", sinkn_in, sinkn_ref)
    fetch("reach", reach_in, reach_ref)
    fetch("gain", ng, gain)
    for q in range(REQ):
        fetch(("hid", q), hid.at[q], xg.at[q, t])
    fetch("wq", qw, wq)
    fetch("wkv", kvw, wkv)
    for q in range(REQ):
        for k in range(2):
            fetch(
                ("win", q, k),
                win.at[q, chip, :, k * HD : (k + 1) * HD],
                kvb.at[k, q, slots(t)],
            )
    fetch("sink", sink.at[:, chip], sinkb)
    fetch("wo0", ow.at[:, columns(t)], wo.at[core, 0])
    fetch("wo1", ow.at[:, columns(to)], wo.at[core, 1])
    fetch("pg", pg, pgain)

    pl.semaphore_wait(barrier, 3)

    pieces = [(q, h) for q in range(REQ) for h in range(2)]

    def send_rows(q, h):
        rows = pl.ds(h * HALF, HALF)
        make(("H", q, h), hid.at[q, rows], xg.at[q, t, rows], to).start()

    def send_cache(q):
        for k in range(2):
            lanes = slice(k * HD, (k + 1) * HD)
            make(("C", q, k), win.at[q, other, :, lanes], kvb.at[k, q, slots(t)], to).start()

    send_rows(0, 0)
    send_rows(0, 1)
    send_cache(0)
    send_rows(1, 0)
    send_cache(1)
    send_rows(1, 1)
    for q in range(REQ):
        make(("D", q), hid.at[q], xg.at[q, t], tc).start()
    for q in range(REQ):
        for k in range(2):
            lanes = slice(k * HD, (k + 1) * HD)
            make(("E", q, k), win.at[q, chip, :, lanes], kvb.at[k, q, slots(t)], tc).start()
    make(("W", 0), ow.at[:, columns(tc)], wo.at[core, 0], tc).start()
    make(("W", 1), ow.at[:, columns(tx)], wo.at[core, 1], tc).start()
    for q, h in pieces:
        rows = pl.ds(h * HALF, HALF)
        make(("HF", q, h), xg.at[q, to, rows], xg.at[q, to, rows], tc)
        new_rows = pl.ds(NEW + h * HALF, HALF)
        make(("N", q, h), kvb.at[core, q, new_rows], kvb.at[core, q, new_rows], tc)
        make(("A", q, h), attb.at[q, core, rows], attb.at[q, core, rows], tc)
    for i, (q, h, first, count) in enumerate(OUTS):
        rows = pl.ds(first, count)
        make(("O", i), sendb.at[q, h, rows], recvb.at[q, h, rows], to)
        for name, peer in (("o", to), ("x", tx), ("c", tc)):
            make(("S" + name, i), ssb.at[i, t], ssb.at[i, t], peer)
    for q in range(REQ):
        for k in range(2):
            make(("CF", q, k), kvb.at[k, q, slots(to)], kvb.at[k, q, slots(to)], tc)

    for name in ("cached", "span", "sinkn", "reach"):
        local[name].wait()
    lane = lax.broadcasted_iota(jnp.int32, (HALF, HD // 2), 1).astype(F32)
    frequency = jnp.exp(lane * (-2.0 * math.log(10000.0) / HD))
    for q, h in pieces:
        row = lax.broadcasted_iota(jnp.int32, (HALF, HD // 2), 0) + h * HALF
        angles = (row + cached_ref[q]).astype(F32) * frequency
        cosb[q, h] = jnp.cos(angles)
        sinb[q, h] = jnp.sin(angles)
    for q, h in pieces:
        cached, fresh, sinks, reach = cached_ref[q], span_ref[q], sinkn_ref[q], reach_ref[q]
        row = lax.broadcasted_iota(jnp.int32, (HALF, WIN), 0) + h * HALF
        col = lax.broadcasted_iota(jnp.int32, (HALF, WIN), 1)
        allowed = (col >= sinks + WIN - cached) & (row + WIN - col < reach)
        biasb[q, h, :, PAD:NEW] = jnp.where(allowed, 0.0, NEG)
        row = lax.broadcasted_iota(jnp.int32, (HALF, SPAN), 0) + h * HALF
        col = lax.broadcasted_iota(jnp.int32, (HALF, SPAN), 1)
        allowed = (col <= row) & (col < fresh) & (row - col < reach)
        biasb[q, h, :, NEW:COLS] = jnp.where(allowed, 0.0, NEG)
        col = lax.broadcasted_iota(jnp.int32, (HALF, PAD), 1)
        biasb[q, h, :, 0:PAD] = jnp.where(col < jnp.minimum(sinks, SINK), 0.0, NEG)
    local["sink"].wait()
    for q in range(REQ):
        for k in range(2):
            kvb[k, q, 0:PAD, :] = jnp.zeros((PAD, HD), BF16)
            kvb[k, q, 0:SINK, :] = sinkb[q, :, k * HD : (k + 1) * HD]
    local["gain"].wait()
    local["wq"].wait()
    local["wkv"].wait()

    def pass_on(q, h):
        remote["H", q, h].wait_recv()
        remote["HF", q, h].start()

    def pass_cache(q):
        for k in range(2):
            remote["C", q, k].wait_recv()
            remote["CF", q, k].start()

    def project(q, h):
        rows = slice(h * HALF, (h + 1) * HALF)
        if h == 0:
            local["hid", q].wait()
            remote["D", q].wait_recv()
        remote["HF", q, h].wait_recv()
        square = jnp.zeros((HALF, 1), F32)
        acc_q = jnp.zeros((HALF, 2 * HD), F32)
        acc_kv = jnp.zeros((HALF, HD), F32)
        for s in range(TP):
            span = slice(s * FEAT, (s + 1) * FEAT)
            x = xg[q, s, rows, :].astype(F32)
            square += jnp.sum(x * x, axis=-1, keepdims=True)
            scaled = (x * gain[:, span]).astype(BF16)
            acc_q += jnp.dot(scaled, wq[span, :], preferred_element_type=F32)
            acc_kv += jnp.dot(scaled, wkv[span, :], preferred_element_type=F32)
        scale = lax.rsqrt(square * (1.0 / D) + EPS)
        cosine, sine = cosb[q, h], sinb[q, h]
        cosine, sine = cosine * scale, sine * scale
        u, w = acc_kv[:, : HD // 2], acc_kv[:, HD // 2 :]
        is_key = core == 0
        cos_kv = jnp.where(is_key, cosine, jnp.broadcast_to(scale, cosine.shape))
        sin_kv = jnp.where(is_key, sine, 0.0)
        new_rows = slice(NEW + h * HALF, NEW + (h + 1) * HALF)
        kvb[core, q, new_rows, : HD // 2] = (u * cos_kv - w * sin_kv).astype(BF16)
        kvb[core, q, new_rows, HD // 2 :] = (w * cos_kv + u * sin_kv).astype(BF16)
        remote["N", q, h].start()
        cosine, sine = cosine * (1.0 / math.sqrt(HD)), sine * (1.0 / math.sqrt(HD))
        for n in range(2):
            u = acc_q[:, n * HD : n * HD + HD // 2]
            w = acc_q[:, n * HD + HD // 2 : (n + 1) * HD]
            qb[q, h, n, :, : HD // 2] = (u * cosine - w * sine).astype(BF16)
            qb[q, h, n, :, HD // 2 :] = (w * cosine + u * sine).astype(BF16)

    def keys_ready(q):
        for k in range(2):
            local["win", q, k].wait()
            remote["E", q, k].wait_recv()
            remote["CF", q, k].wait_recv()

    def attend(q, h):
        remote["N", q, h].wait_recv()
        cols = NEW + (h + 1) * HALF
        query = qb[q, h].reshape(2 * HALF, HD)
        scores = lax.dot_general(
            query, kvb[0, q, :cols], (((1,), (1,)), ((), ())), preferred_element_type=F32
        )
        scores = scores.reshape(2, HALF, cols) + biasb[q, h, :, :cols][None]
        peak = jnp.max(scores, axis=-1, keepdims=True)
        weights = jnp.exp(scores - peak)
        total = jnp.sum(weights, axis=-1, keepdims=True).reshape(2 * HALF, 1)
        weights = weights.astype(BF16).reshape(2 * HALF, cols)
        mixed = jnp.dot(weights, kvb[1, q, :cols], preferred_element_type=F32) * (1.0 / total)
        mixed = mixed.astype(BF16)
        rows = slice(h * HALF, (h + 1) * HALF)
        for n in range(2):
            attb[q, core, rows, n * HD : (n + 1) * HD] = mixed[n * HALF : (n + 1) * HALF]
        remote["A", q, h].start()

    def emit(q, h):
        rows = slice(h * HALF, (h + 1) * HALF)
        remote["A", q, h].wait_recv()
        first, second = attb[q, 0, rows, :], attb[q, 1, rows, :]
        lent = jnp.dot(first, wo[0, 1], preferred_element_type=F32) + jnp.dot(
            second, wo[1, 1], preferred_element_type=F32
        )
        sendb[q, h] = lent.astype(BF16)
        for i, piece in enumerate(OUTS):
            if piece[:2] == (q, h):
                remote["O", i].start()
        ownb[q, h] = jnp.dot(first, wo[0, 0], preferred_element_type=F32) + jnp.dot(
            second, wo[1, 0], preferred_element_type=F32
        )

    def diagonal(count):
        row = lax.broadcasted_iota(jnp.int32, (count, 128), 0)
        return row == lax.broadcasted_iota(jnp.int32, (count, 128), 1)

    def squares(i):
        q, h, first, count = OUTS[i]
        rows = slice(first, first + count)
        remote["O", i].wait_recv()
        projected = ownb[q, h, rows, :] + recvb[q, h, rows, :].astype(F32)
        ownb[q, h, rows, :] = projected
        square = jnp.sum(projected * projected, axis=-1, keepdims=True)
        turned = jnp.sum(jnp.where(diagonal(count), square, 0.0), axis=0, keepdims=True)
        ssb[i, t] = jnp.broadcast_to(turned, (8, 128))
        for name in ("So", "Sx", "Sc"):
            remote[name, i].start()

    def finish(i):
        q, h, first, count = OUTS[i]
        for name in ("So", "Sx", "Sc"):
            remote[name, i].wait_recv()
        square = ssb[i, 0] + ssb[i, 1] + ssb[i, 2] + ssb[i, 3]
        scale = lax.rsqrt(square * (1.0 / D) + EPS)[0:1, :]
        scale = jnp.sum(jnp.where(diagonal(count), scale, 0.0), axis=-1, keepdims=True)
        rows = slice(h * HALF + first, h * HALF + first + count)
        kept = xg[q, t, rows, :].astype(F32)
        projected = ownb[q, h, first : first + count, :]
        out[q, rows, :] = (kept + pgain[...] * projected * scale).astype(BF16)

    pass_on(0, 0)
    project(0, 0)
    pass_on(0, 1)
    project(0, 1)
    pass_cache(0)
    keys_ready(0)
    attend(0, 0)
    attend(0, 1)
    pass_on(1, 0)
    for name in ("wo0", "wo1", "pg"):
        local[name].wait()
    for i in range(2):
        remote["W", i].wait_recv()
    emit(0, 0)
    emit(0, 1)
    project(1, 0)
    pass_cache(1)
    keys_ready(1)
    attend(1, 0)
    pass_on(1, 1)
    emit(1, 0)
    project(1, 1)
    attend(1, 1)
    emit(1, 1)
    for i in range(len(OUTS)):
        squares(i)
        if i == 2:
            finish(0)
            finish(1)
    for i in range(2, len(OUTS)):
        finish(i)
    for copy in remote.values():
        copy.wait_send()


def per_device(
    hidden_in,
    norm_gain,
    q_weight,
    kv_weight,
    out_weight,
    post_gain,
    sink_cache,
    window_cache,
    cached_len,
    span_len,
    sink_count,
    window_size,
):
    anywhere = pl.BlockSpec(memory_space=pl.ANY)
    copies = 70
    return pl.pallas_call(
        layer_kernel,
        out_shape=pltpu.VMEM((REQ, SPAN, FEAT), BF16),
        in_specs=[anywhere] * 12,
        out_specs=pl.BlockSpec(memory_space=pltpu.VMEM),
        scratch_shapes=[
            pltpu.SMEM((REQ,), jnp.int32),
            pltpu.SMEM((REQ,), jnp.int32),
            pltpu.SMEM((REQ,), jnp.int32),
            pltpu.SMEM((REQ,), jnp.int32),
            pltpu.VMEM((REQ, TP, SPAN, FEAT), BF16),
            pltpu.VMEM((D, 2 * HD), BF16),
            pltpu.VMEM((D, HD), BF16),
            pltpu.VMEM((2, 2, 2 * HD, FEAT), BF16),
            pltpu.VMEM((1, D), F32),
            pltpu.VMEM((1, FEAT), F32),
            pltpu.VMEM((REQ, SINK, 2 * HD), BF16),
            pltpu.VMEM((2, REQ, COLS, HD), BF16),
            pltpu.VMEM((REQ, 2, 2, HALF, HD), BF16),
            pltpu.VMEM((REQ, 2, HALF, COLS), F32),
            pltpu.VMEM((REQ, 2, HALF, HD // 2), F32),
            pltpu.VMEM((REQ, 2, HALF, HD // 2), F32),
            pltpu.VMEM((REQ, 2, SPAN, 2 * HD), BF16),
            pltpu.VMEM((REQ, 2, HALF, FEAT), F32),
            pltpu.VMEM((REQ, 2, HALF, FEAT), BF16),
            pltpu.VMEM((REQ, 2, HALF, FEAT), BF16),
            pltpu.VMEM((len(OUTS), TP, 8, 128), F32),
            pltpu.SemaphoreType.DMA((20,)),
            pltpu.SemaphoreType.DMA((copies,)),
            pltpu.SemaphoreType.DMA((copies,)),
        ],
        compiler_params=pltpu.CompilerParams(
            collective_id=0, has_side_effects=True, vmem_limit_bytes=60 * 2**20
        ),
    )(
        cached_len,
        span_len,
        sink_count,
        window_size,
        hidden_in,
        norm_gain.reshape(1, D),
        q_weight,
        kv_weight,
        out_weight,
        post_gain.reshape(1, FEAT),
        sink_cache,
        window_cache,
    )


def solution(mesh):
    in_specs = (
        P("req", None, "tp"),
        P(),
        P(None, "tp"),
        P(None, "tp"),
        P("tp", None),
        P("tp"),
        P("req", None, None, None),
        P("req", None, "tp", None),
        P("req"),
        P("req"),
        P("req"),
        P("req"),
    )
    return jax.shard_map(
        per_device,
        mesh=mesh,
        in_specs=in_specs,
        out_specs=P("req", None, "tp"),
        check_vma=False,
    )
```
